1024 devices in a mesh: row: 8 (over x_lo, core), col: 128 (over x_hi, y, z).
Axes of the slice: x: 8 (x_hi: 2, x_lo: 4; x = x_hi * 4 + x_lo), y: 8, z: 8, core: 2. Of those that a mesh axis runs over, the one named last changes fastest.
Arguments:
- blocks: float32 [8, 128, 4, 128, 128], P('row', 'col')
- block_rows: int32 [8, 128, 4], P('row', 'col'), may hold values from 0 to 31, as said below
- block_cols: int32 [8, 128, 4], P('row', 'col'), may hold values from 0 to 7
- counts: int32 [8, 128], P('row', 'col'), may hold values from 2 to 4, as said below
- x_prev: float32 [131072], P('col'), may hold values from 0 to 1
- y_prev: float32 [32768], P('row'), may hold values from -6 to 6
- cost: float32 [131072], P('col'), may hold values from -6 to 6
- rhs: float32 [32768], P('row'), may hold values from -6 to 6
- upper: float32 [131072], P('col'), may hold values from 0.5 to 4
- steps: float32 [2], replicated, may hold values from 0.1 to 0.4
Outputs:
- x_new: float32 [131072], P('col')
- y_new: float32 [32768], P('row')
- stats: float32 [3], replicated
The draws below stay inside these ranges and needn't reach their ends.
Inputs may be any that keep to these rules, and one draw needn't show every extreme that they name: `block_rows`: pairs of block row and block column may repeat within a device. `counts`: stored blocks at positions from the count on are padding and are not part of the matrix; some device holds 4 live blocks in every draw.
All inputs are finite; a program needn't handle non-finite values.
Results may differ from the reference program's by a relative error of at most 0.00011.
Values sent between devices are 32-bit elements; how exact they have to be, the bound alone decides.
A program may use at most 32 MiB of HBM per device.

```python
import math
import jax
import jax.numpy as jnp
from jax import lax

BS = 128
RB = 32
CB = 8
NBD = 4
NRG = 8
NCG = 128
M = 32768
N = 131072


def pattern(key):
    rows = jax.random.randint(jax.random.fold_in(key, 11), (NRG, NCG, NBD), 0, RB)
    cols = jax.random.randint(jax.random.fold_in(key, 12), (NRG, NCG, NBD), 0, CB)
    return (rows, cols)


def draw_block_rows(key, part):
    return pattern(key)[0].astype(jnp.int32)


def draw_block_cols(key, part):
    return pattern(key)[1].astype(jnp.int32)


def draw_counts(key, part):
    base = jax.random.randint(jax.random.fold_in(key, 21), (NRG * NCG,), NBD // 2, NBD + 1)
    pick = jax.random.randint(jax.random.fold_in(key, 22), (), 0, NRG * NCG)
    full = jnp.where(jnp.arange(NRG * NCG) == pick, NBD, base)
    return full.reshape(NRG, NCG).astype(jnp.int32)


def draw_blocks(key, part):
    rows, cols = pattern(key)
    grow = jnp.arange(NRG)[:, None, None] * RB + rows
    gcol = jnp.arange(NCG)[None, :, None] * CB + cols
    low = jnp.log(0.05)
    high = jnp.log(2.0)
    entries = jax.random.normal(jax.random.fold_in(key, 31), (NRG, NCG, NBD, BS, BS), jnp.float32)
    row_scale = jnp.exp(jax.random.uniform(jax.random.fold_in(key, 32), (NRG * RB, BS), jnp.float32, low, high))
    col_scale = jnp.exp(jax.random.uniform(jax.random.fold_in(key, 33), (NCG * CB, BS), jnp.float32, low, high))
    return (entries * row_scale[grow][..., :, None] * col_scale[gcol][..., None, :]).astype(jnp.float32)


def levels(own_key, shape, shards, low, top_value):
    gain, own = 1.0, jax.random.fold_in(own_key, 6)
    for position, shards_of in shards:
        heights = jnp.exp(jax.random.uniform(jax.random.fold_in(own, position), (shards_of,), jnp.float32, low / len(shards), top_value / len(shards)))
        gain = gain * jnp.repeat(heights, shape[position] // shards_of).reshape([-1 if axis == position else 1 for axis in range(len(shape))])
    return gain


def normal_values(stream_key, shape, deviation, bound, split=(), kind=jnp.bfloat16):
    result = jax.random.normal(stream_key, shape, jnp.float32) * deviation
    if len(split) > 0:
        result = levels(stream_key, shape, split, -0.22, 0.18) * result
    return jnp.clip(result, min=-bound, max=bound).astype(kind)


def setup_inputs(seed: int = 0) -> dict:
    splits = jax.random.split(jax.random.key(seed), 11)
    return {
        "blocks": draw_blocks(jax.random.fold_in(splits[10], 71), 0),
        "block_rows": draw_block_rows(jax.random.fold_in(splits[10], 71), 0),
        "block_cols": draw_block_cols(jax.random.fold_in(splits[10], 71), 0),
        "counts": draw_counts(jax.random.fold_in(splits[10], 71), 0),
        "x_prev": jnp.clip(1.0 * jax.random.uniform(splits[4], (N,), jnp.float32) ** levels(splits[4], (N,), ((0, 128),), -0.2, 0.2), 0.0, 1.0),
        "y_prev": normal_values(splits[5], (M,), 1.0, 6.0, ((0, 8),), jnp.float32),
        "cost": normal_values(splits[6], (N,), 1.0, 6.0, ((0, 128),), jnp.float32),
        "rhs": normal_values(splits[7], (M,), 1.0, 6.0, ((0, 8),), jnp.float32),
        "upper": jnp.clip(jnp.exp(math.log(4.0) - 2.0794415 * jax.random.uniform(splits[8], (N,), jnp.float32) ** levels(splits[8], (N,), ((0, 128),), -0.2, 0.2)), 0.5, 4.0),
        "steps": jnp.clip(jax.random.uniform(splits[9], (2,), jnp.float32, 0.1, 0.4), 0.1, 0.4),
    }


def reference(blocks, block_rows, block_cols, counts, x_prev, y_prev, cost, rhs, upper, steps):
    nbd = blocks.shape[2]
    live = (jnp.arange(nbd, dtype=jnp.int32)[None, None, :] < counts[:, :, None]).astype(jnp.float32).reshape(-1)
    grow = (jnp.arange(NRG, dtype=jnp.int32)[:, None, None] * RB + block_rows).reshape(-1)
    gcol = (jnp.arange(NCG, dtype=jnp.int32)[None, :, None] * CB + block_cols).reshape(-1)
    flat = blocks.reshape(-1, BS, BS)
    rpeak = lax.optimization_barrier(jnp.max(jnp.abs(flat), axis=2)) * live[:, None]
    cpeak = lax.optimization_barrier(jnp.max(jnp.abs(flat), axis=1)) * live[:, None]
    rowmax = jnp.maximum(jax.ops.segment_max(rpeak, grow, num_segments=NRG * RB), 0.0).reshape(-1)
    colmax = jnp.maximum(jax.ops.segment_max(cpeak, gcol, num_segments=NCG * CB), 0.0).reshape(-1)
    row_scale = 1.0 / jnp.sqrt(jnp.maximum(rowmax, 0.5))
    col_scale = 1.0 / jnp.sqrt(jnp.maximum(colmax, 0.5))

    def forward(vecs):
        count = vecs.shape[0]
        picked = (vecs * col_scale[None, :]).reshape(count, NCG * CB, BS)[:, gcol]
        prod = jnp.einsum('kij,vkj->kvi', flat, picked, precision=lax.Precision.HIGHEST) * live[:, None, None]
        summed = jax.ops.segment_sum(prod, grow, num_segments=NRG * RB)
        return jnp.transpose(summed, (1, 0, 2)).reshape(count, -1) * row_scale[None, :]

    def backward(vec):
        picked = (vec * row_scale).reshape(NRG * RB, BS)[grow]
        prod = jnp.einsum('kij,ki->kj', flat, picked, precision=lax.Precision.HIGHEST) * live[:, None]
        return jax.ops.segment_sum(prod, gcol, num_segments=NCG * CB).reshape(-1) * col_scale
    cost_s = col_scale * cost
    rhs_s = row_scale * rhs
    upper_s = upper / col_scale
    eta = steps[0]
    omega = steps[1]
    tau = eta / omega
    sigma = eta * omega
    grad = cost_s - backward(y_prev)
    x_new = jnp.clip(x_prev - tau * grad, 0.0, upper_s)
    delta_x = x_new - x_prev
    both = forward(jnp.stack([x_new, delta_x]))
    ax_new = both[0]
    adx = both[1]
    y_new = y_prev + sigma * (rhs_s - ax_new - adx)
    delta_y = y_new - y_prev
    reduced = cost_s - backward(y_new)
    resid = rhs_s - ax_new
    dx2 = jnp.sum(delta_x * delta_x)
    cx = jnp.sum(cost_s * x_new)
    uneg = jnp.sum(upper_s * jnp.maximum(-reduced, 0.0))
    dy2 = jnp.sum(delta_y * delta_y)
    adx2 = jnp.sum(adx * adx)
    res2 = jnp.sum(resid * resid)
    by = jnp.sum(rhs_s * y_new)
    movement = 0.5 * omega * dx2 + 0.5 / omega * dy2
    stats = jnp.stack([jnp.sqrt(res2 / M), (cx - by + uneg) / N, movement / jnp.sqrt(adx2 * dy2 + 1e-06)])
    return (x_new, y_new, stats)
```

```python
import functools

import jax
import jax.numpy as jnp
from jax import lax
from jax.experimental import pallas as pl
from jax.experimental.pallas import tpu as pltpu
from jax.sharding import PartitionSpec as P

MESH = pl.DeviceIdType.MESH
LANES = 128
COL_GRID = {128: (2, 8, 8), 8: (2, 2, 2)}
STOP = 99


def far_first(n):
    return sorted(range(1, n), key=lambda d: -min(d, n - d))


def total(terms, op):
    acc = terms[0]
    for term in terms[1:]:
        acc = op(acc, term)
    return acc


def body(
    grid, nrow, nbd,
    brow_ref, bcol_ref, count_ref, steps_ref, blocks_ref, x_ref, y_ref, cost_ref, rhs_ref, upper_ref,
    x_out, y_out, stats_out,
    flip_ref, scaled_ref, vec_ref,
    max_send, max_y, max_z, max_x, max_all, cmax_buf,
    part_buf, fwd_send, fwd_y, fwd_z, fwd_x, fwd_all, dual_buf, back_buf, sum_y, sum_z, sum_x,
    send_sems, recv_sems,
):
    nx, ny, nz = grid
    rb = y_ref.shape[0]
    cb = x_ref.shape[0]
    share = rb // ny
    row = lax.axis_index("row")
    col = lax.axis_index("col")
    xh = col // (ny * nz)
    yi = (col // nz) % ny
    zi = col % nz

    def y_peer(d):
        other = (yi + d) % ny
        return (row, (xh * ny + other) * nz + zi), other

    def z_peer(d):
        other = (zi + d) % nz
        return (row, (xh * ny + yi) * nz + other), other

    def x_peer(d):
        other = (xh + d) % nx
        return (row, (other * ny + yi) * nz + zi), other

    def r_peer(d):
        other = (row + d) % nrow
        return (other, col), other

    lines = {"y": (y_peer, yi, ny), "z": (z_peer, zi, nz), "x": (x_peer, xh, nx), "r": (r_peer, row, nrow)}
    barrier = pltpu.get_barrier_semaphore()
    greeted = 0
    for peer, _, n in lines.values():
        for d in far_first(n):
            pl.semaphore_signal(barrier, inc=1, device_id=peer(d)[0], device_id_type=MESH)
            greeted += 1

    used = [0]
    pending = []

    def send(axis, buf, source=None):
        peer, me, n = lines[axis]
        base = used[0]
        used[0] += n - 1
        for d in far_first(n):
            device, other = peer(d)
            copy = pltpu.make_async_remote_copy(
                src_ref=buf.at[me] if source is None else source(other),
                dst_ref=buf.at[me],
                send_sem=send_sems.at[base + d - 1],
                recv_sem=recv_sems.at[base + d - 1],
                device_id=device,
                device_id_type=MESH,
            )
            copy.start()
            pending.append(copy)

        def arrive():
            for d in far_first(n)[::-1]:
                device, other = peer(n - d)
                pltpu.make_async_remote_copy(
                    src_ref=buf.at[other],
                    dst_ref=buf.at[other],
                    send_sem=send_sems.at[base + d - 1],
                    recv_sem=recv_sems.at[base + d - 1],
                    device_id=device,
                    device_id_type=MESH,
                ).wait_recv()

        return arrive

    def whole(buf, op):
        return total([buf[i] for i in range(buf.shape[0])], op)

    count = count_ref[0]
    rows = [jnp.where(k < count, brow_ref[k], -1) for k in range(nbd)]
    cols = [jnp.where(k < count, bcol_ref[k], -1) for k in range(nbd)]
    share_at = lax.broadcasted_iota(jnp.int32, (share, LANES), 0)
    cb_at = lax.broadcasted_iota(jnp.int32, (cb, LANES), 0)

    col_peak = jnp.zeros((cb, LANES), jnp.float32)
    row_peaks = []
    for k in range(nbd):
        block = blocks_ref[k]
        flip = block.T
        flip_ref[k] = flip
        row_peaks.append(jnp.max(jnp.abs(flip), axis=0, keepdims=True))
        peak = jnp.max(jnp.abs(block), axis=0, keepdims=True)
        col_peak = jnp.maximum(col_peak, jnp.where(cb_at == cols[k], peak, 0.0))
    for j in range(ny):
        max_send[j] = total(
            [jnp.where(share_at + j * share == rows[k], row_peaks[k], 0.0) for k in range(nbd)], jnp.maximum
        )
    cmax_buf[row] = col_peak
    max_y[yi] = max_send[yi]
    pl.semaphore_wait(barrier, greeted)
    if STOP <= 0:
        return

    arrive_y = send("y", max_y, lambda other: max_send.at[other])
    arrive_c = send("r", cmax_buf)
    arrive_y()
    max_z[zi] = whole(max_y, jnp.maximum)
    arrive = send("z", max_z)
    arrive_c()
    col_scale = 1.0 / jnp.sqrt(jnp.maximum(whole(cmax_buf, jnp.maximum), 0.5))
    arrive()
    max_x[xh] = whole(max_z, jnp.maximum)
    send("x", max_x)()
    row_scale = 1.0 / jnp.sqrt(jnp.maximum(whole(max_x, jnp.maximum), 0.5))
    max_all[yi] = row_scale
    send("y", max_all)()

    def picked(read):
        got = jnp.concatenate([read(brow_ref[k]) for k in range(nbd)] * (8 // nbd), axis=0)
        return got.T

    def scale_of(at):
        return max_all[at // share, pl.ds(at % share, 1), :]

    def backward(read):
        vec = picked(lambda at: read(at) * scale_of(at))
        out = jnp.zeros((cb, LANES), jnp.float32)
        for k in range(nbd):
            prod = jnp.sum(blocks_ref[k] * vec[:, k : k + 1], axis=0, keepdims=True)
            out = out + jnp.where(cb_at == cols[k], prod, 0.0)
        return out

    eta = steps_ref[0]
    omega = steps_ref[1]
    omega_v = jnp.full((1, 1), omega)
    tau = eta / omega_v
    sigma = eta * omega

    part_buf[row] = backward(lambda at: y_ref[pl.ds(at, 1), :])
    send("r", part_buf)()
    cost_s = col_scale * cost_ref[...]
    upper_s = upper_ref[...] / col_scale
    x_prev = x_ref[...]
    grad = cost_s - whole(part_buf, jnp.add) * col_scale
    x_new = jnp.clip(x_prev - tau * grad, 0.0, upper_s)
    delta_x = x_new - x_prev
    x_out[...] = x_new
    vec_ref[0] = x_new * col_scale
    vec_ref[1] = delta_x * col_scale

    vecs = jnp.concatenate(
        [vec_ref[v, pl.ds(bcol_ref[k], 1), :] for v in range(2) for k in range(nbd)], axis=0
    ).T
    pair_at = lax.broadcasted_iota(jnp.int32, (2 * share, LANES), 0)
    pair_row = pair_at % share
    prods = []
    for k in range(nbd):
        flip = flip_ref[k]
        ax = jnp.sum(flip * vecs[:, k : k + 1], axis=0, keepdims=True)
        adx = jnp.sum(flip * vecs[:, nbd + k : nbd + k + 1], axis=0, keepdims=True)
        prods.append(jnp.where(pair_at < share, ax, adx))
    for j in range(ny):
        fwd_send[j] = total(
            [jnp.where(pair_row + j * share == rows[k], prods[k], 0.0) for k in range(nbd)], jnp.add
        )
    fwd_y[yi] = fwd_send[yi]
    send("y", fwd_y, lambda other: fwd_send.at[other])()
    fwd_z[zi] = whole(fwd_y, jnp.add)
    send("z", fwd_z)()
    fwd_x[xh] = whole(fwd_z, jnp.add)
    send("x", fwd_x)()
    pair = whole(fwd_x, jnp.add)
    ax = pair[:share] * row_scale
    adx = pair[share:] * row_scale
    start = pl.multiple_of(yi * share, share)
    rhs_s = row_scale * rhs_ref[yi]
    y_prev = y_ref[pl.ds(start, share), :]
    y_new = y_prev + sigma * (rhs_s - ax - adx)
    delta_y = y_new - y_prev
    resid = rhs_s - ax
    fwd_all[yi, :share] = y_new
    for at, term in enumerate((delta_y * delta_y, adx * adx, resid * resid, rhs_s * y_new)):
        fwd_all[yi, share + at : share + at + 1] = jnp.sum(term, axis=0, keepdims=True)
    send("y", fwd_all)()
    dual_buf[row] = total([fwd_all[j, share : share + 4] for j in range(ny)], jnp.add)
    arrive_dual = send("r", dual_buf)
    for j in range(ny):
        y_out[j * share : (j + 1) * share] = fwd_all[j, :share]
    back_buf[row] = backward(lambda at: fwd_all[at // share, pl.ds(at % share, 1), :])
    arrive = send("r", back_buf)
    arrive_dual()
    dual = jnp.sum(whole(dual_buf, jnp.add), axis=1, keepdims=True)
    arrive()
    reduced = cost_s - whole(back_buf, jnp.add) * col_scale
    slot = lax.broadcasted_iota(jnp.int32, (8, LANES), 0)
    terms = [
        jnp.sum(term, axis=0, keepdims=True)
        for term in (delta_x * delta_x, cost_s * x_new, upper_s * jnp.maximum(-reduced, 0.0))
    ]
    sum_y[yi] = jnp.where(slot == 0, terms[0], jnp.where(slot == 1, terms[1], jnp.where(slot == 2, terms[2], 0.0)))
    send("y", sum_y)()
    sum_z[zi] = whole(sum_y, jnp.add)
    send("z", sum_z)()
    sum_x[xh] = whole(sum_z, jnp.add)
    send("x", sum_x)()
    primal = jnp.sum(whole(sum_x, jnp.add), axis=1, keepdims=True)
    dx2, cx, uneg = primal[0:1], primal[1:2], primal[2:3]
    dy2, adx2, res2, by = dual[0:1], dual[1:2], dual[2:3], dual[3:4]
    m = rb * LANES * nrow
    n = cb * LANES * nx * ny * nz
    movement = 0.5 * omega * dx2 + 0.5 / omega_v * dy2
    lane = lax.broadcasted_iota(jnp.int32, (1, LANES), 1)
    stats_out[...] = jnp.where(
        lane == 0,
        jnp.sqrt(res2 / m),
        jnp.where(lane == 1, (cx - by + uneg) / n, movement / jnp.sqrt(adx2 * dy2 + 1e-06)),
    )
    for copy in pending:
        copy.wait_send()


def shards(grid, nrow, blocks, block_rows, block_cols, counts, x_prev, y_prev, cost, rhs, upper, steps):
    nx, ny, nz = grid
    nbd, bsz = blocks.shape[2], blocks.shape[3]
    rb = y_prev.shape[0] // bsz
    cb = x_prev.shape[0] // bsz
    share = rb // ny
    copies = 4 * (ny - 1) + 3 * (nz - 1) + 3 * (nx - 1) + 4 * (nrow - 1) + (ny - 1)
    vmem = pl.BlockSpec(memory_space=pltpu.VMEM)
    smem = pl.BlockSpec(memory_space=pltpu.SMEM)
    f32 = jnp.float32

    def buf(n, rows):
        return pltpu.VMEM((n, rows, LANES), f32)

    x_new, y_new, stats = pl.pallas_call(
        functools.partial(body, grid, nrow, nbd),
        out_shape=(
            jax.ShapeDtypeStruct((cb, bsz), f32),
            jax.ShapeDtypeStruct((rb, bsz), f32),
            jax.ShapeDtypeStruct((1, LANES), f32),
        ),
        in_specs=[smem] * 4 + [vmem] * 6,
        out_specs=(vmem, vmem, vmem),
        scratch_shapes=[
            pltpu.VMEM((nbd, bsz, bsz), f32),
            buf(ny, share),
            buf(2, cb),
            buf(ny, share), buf(ny, share), buf(nz, share), buf(nx, share), buf(ny, share), buf(nrow, cb),
            buf(nrow, cb), buf(ny, 2 * share), buf(ny, 2 * share), buf(nz, 2 * share), buf(nx, 2 * share),
            buf(ny, 2 * share), buf(nrow, 4), buf(nrow, cb), buf(ny, 8), buf(nz, 8), buf(nx, 8),
            pltpu.SemaphoreType.DMA((copies,)),
            pltpu.SemaphoreType.DMA((copies,)),
        ],
        compiler_params=pltpu.CompilerParams(collective_id=0, has_side_effects=True),
        name="pdlp",
    )(
        block_rows.reshape(nbd),
        block_cols.reshape(nbd),
        counts.reshape(1),
        steps,
        blocks.reshape(nbd, bsz, bsz),
        x_prev.reshape(cb, bsz),
        y_prev.reshape(rb, bsz),
        cost.reshape(cb, bsz),
        rhs.reshape(ny, share, bsz),
        upper.reshape(cb, bsz),
    )
    return x_new.reshape(-1), y_new.reshape(-1), stats[0, :3]


def solution(mesh):
    placed = (
        P("row", "col", None, None, None),
        P("row", "col", None),
        P("row", "col", None),
        P("row", "col"),
        P("col"),
        P("row"),
        P("col"),
        P("row"),
        P("col"),
        P(),
    )
    return jax.shard_map(
        functools.partial(shards, COL_GRID[mesh.shape["col"]], mesh.shape["row"]),
        mesh=mesh,
        in_specs=placed,
        out_specs=(P("col"), P("row"), P()),
        check_vma=False,
    )
```

```python
import functools

import jax
import jax.numpy as jnp
from jax import lax
from jax.experimental import pallas as pl
from jax.experimental.pallas import tpu as pltpu
from jax.sharding import PartitionSpec as P

MESH = pl.DeviceIdType.MESH
LANES = 128
NOWHERE = 1000.0
COL_GRID = {128: (2, 8, 8), 16: (2, 4, 2)}


def hops(d, n):
    return min(d, n - d)


def far_first(n):
    return sorted(range(1, n), key=lambda d: -hops(d, n))


def total(terms, op):
    acc = terms[0]
    for term in terms[1:]:
        acc = op(acc, term)
    return acc


def body(
    grid, nrow, nbd,
    brow_hbm, bcol_hbm, count_hbm, steps_hbm, blocks_hbm, x_hbm, y_hbm, cost_hbm, rhs_hbm, upper_hbm,
    x_out, y_out, stats_out,
    brow_ref, bcol_ref, count_ref, steps_ref, blocks_ref, x_ref, y_ref, cost_ref, rhs_ref, upper_ref,
    flip_ref, vec_ref, scale_ref, hot_ref,
    max_y, max_q, cmax_buf, part_buf, fwd_buf, dual_buf, back_buf, sum_buf,
    local_sems, send_sems, recv_sems, reached,
):
    nx, ny, nz = grid
    rb = y_ref.shape[0]
    cb = x_ref.shape[0]
    nq = nx * nz
    ncol = nq * ny
    qlanes = ny * 2 * nbd
    qper = LANES // qlanes
    row = lax.axis_index("row")
    col = lax.axis_index("col")
    xh = lax.div(col, ny * nz)
    yi = lax.rem(lax.div(col, nz), ny)
    zi = lax.rem(col, nz)
    xs = [lax.rem(xh + d, nx) for d in range(nx)]
    ys = [lax.rem(yi + d, ny) for d in range(ny)]
    zs = [lax.rem(zi + d, nz) for d in range(nz)]
    rs = [lax.rem(row + d, nrow) for d in range(nrow)]
    mirror = (nrow // 2 - 1 - lax.div(row, 2)) * 2 + lax.rem(row, 2)
    qi = xh * nz + zi
    slot = qi * ny + yi

    def col_device(d):
        dx, dy, dz = d
        return (row, (xs[dx] * ny + ys[dy]) * nz + zs[dz])

    def mirror_device(d):
        return (mirror if d[0] else row, col_device(d)[1])

    def row_device(d):
        return (rs[d], col)

    def ordered(offsets):
        cost = lambda d: (nx // 2) * 4 * d[0] + hops(d[1], ny) + hops(d[2], nz)
        return sorted(offsets, key=lambda d: -cost(d))

    line_y = [(0, d, 0) for d in far_first(ny)]
    line_z = [(0, 0, d) for d in far_first(nz)]
    plane = ordered([(a, 0, c) for a in range(nx) for c in range(nz) if a or c])
    everyone = ordered([(a, b, c) for a in range(nx) for b in range(ny) for c in range(nz) if a or b or c])
    line_r = far_first(nrow)

    barrier = pltpu.get_barrier_semaphore()
    near = [col_device(d) for d in line_y] + [row_device(d) for d in line_r]
    near += [col_device(d) for d in line_z] + [col_device((1, 0, 0))]
    for device in near:
        pl.semaphore_signal(barrier, inc=1, device_id=device, device_id_type=MESH)
    fetches = [
        pltpu.make_async_copy(src, dst, local_sems.at[i])
        for i, (src, dst) in enumerate(
            (
                (blocks_hbm, blocks_ref), (brow_hbm, brow_ref), (bcol_hbm, bcol_ref), (count_hbm, count_ref),
                (y_hbm, y_ref), (x_hbm, x_ref), (cost_hbm, cost_ref), (rhs_hbm, rhs_ref), (upper_hbm, upper_ref),
                (steps_hbm, steps_ref),
            )
        )
    ]
    for copy in fetches:
        copy.start()
    finish = []

    def send(at, peers, buf, me):
        for device in peers:
            pltpu.make_async_remote_copy(
                src_ref=buf.at[me],
                dst_ref=buf.at[me],
                send_sem=send_sems.at[at],
                recv_sem=recv_sems.at[at],
                device_id=device,
                device_id_type=MESH,
            ).start()
        theirs = buf.at[pl.ds(0, len(peers))]
        finish.append(pltpu.make_async_copy(theirs, theirs, send_sems.at[at]))
        return pltpu.make_async_copy(theirs, theirs, recv_sems.at[at]).wait

    def whole(buf, op):
        return total([buf[i] for i in range(buf.shape[0])], op)

    for copy in fetches[:4]:
        copy.wait()
    count = count_ref[0, 0]
    brow = [brow_ref[0, 0, k] for k in range(nbd)]
    bcol = [bcol_ref[0, 0, k] for k in range(nbd)]
    rows = [jnp.where(k < count, brow[k].astype(jnp.float32), NOWHERE) for k in range(nbd)]
    cols = [jnp.where(k < count, bcol[k], -1) for k in range(nbd)]
    tile_at = lax.broadcasted_iota(jnp.int32, (2 * nbd, LANES), 0)
    cb_at = lax.broadcasted_iota(jnp.int32, (cb, LANES), 0)

    def stacked(entries):
        out = jnp.zeros((len(entries), LANES), jnp.float32)
        for i, entry in enumerate(entries):
            out = jnp.where(tile_at == i, entry, out)
        return out

    col_peak = jnp.zeros((cb, LANES), jnp.float32)
    row_peaks = []
    for k in range(nbd):
        block = blocks_ref[k]
        flip = block.T
        flip_ref[k] = flip
        row_peaks.append(jnp.max(jnp.abs(flip), axis=0, keepdims=True))
        peak = jnp.max(jnp.abs(block), axis=0, keepdims=True)
        col_peak = jnp.maximum(col_peak, jnp.where(cb_at == cols[k], peak, 0.0))
    max_y[yi] = stacked(row_peaks + rows)
    cmax_buf[row] = col_peak
    pl.semaphore_wait(barrier, len(near))
    pl.semaphore_signal(reached, inc=1, device_id=col_device((1, 0, 0)), device_id_type=MESH)
    arrive = send(0, [col_device(d) for d in line_y], max_y, yi)
    arrive_c = send(1, [row_device(d) for d in line_r], cmax_buf, row)
    for copy in fetches[4:]:
        copy.wait()
    arrive()

    rb_at = lax.broadcasted_iota(jnp.int32, (rb, LANES), 0).astype(jnp.float32)
    lane = lax.broadcasted_iota(jnp.int32, (2 * nbd, LANES), 1)
    half = lane % (2 * nbd) // nbd
    mine = (lane // qlanes == lax.rem(qi, qper)) & (tile_at - nbd == lane % nbd)
    owner = lane % qlanes // (2 * nbd)
    dense = jnp.zeros((rb, LANES), jnp.float32)
    codes = jnp.zeros((2 * nbd, LANES), jnp.float32)
    for j in range(ny):
        for k in range(nbd):
            here = rb_at == max_y[j, nbd + k : nbd + k + 1]
            dense = jnp.maximum(dense, jnp.where(here, max_y[j, k : k + 1], 0.0))
        codes = jnp.where(mine & (owner == j), max_y[j], codes)
    codes = jnp.where(mine, codes + (half * rb).astype(jnp.float32), 0.0)
    max_q[qi, :rb] = dense
    max_q[qi, rb:] = jnp.broadcast_to(jnp.sum(codes, axis=0, keepdims=True), (8, LANES))
    pl.semaphore_wait(reached, 1)
    arrive = send(2, [col_device(d) for d in plane], max_q, qi)
    arrive_c()
    col_scale = 1.0 / jnp.sqrt(jnp.maximum(whole(cmax_buf, jnp.maximum), 0.5))
    cost_s = col_scale * cost_ref[...]
    upper_s = upper_ref[...] / col_scale
    x_prev = x_ref[...]
    eta = steps_ref[0]
    omega = steps_ref[1]
    omega_v = jnp.full((1, 1), omega)
    tau = eta / omega_v
    sigma = eta * omega
    arrive()
    rowmax = total([max_q[i, :rb] for i in range(nq)], jnp.maximum)
    row_scale = 1.0 / jnp.sqrt(jnp.maximum(rowmax, 0.5))
    scale_ref[...] = row_scale

    def backward(ref):
        got = [ref[pl.ds(brow[k], 1), :] * scale_ref[pl.ds(brow[k], 1), :] for k in range(nbd)]
        vec = stacked(got + got).T
        out = jnp.zeros((cb, LANES), jnp.float32)
        for k in range(nbd):
            prod = jnp.sum(blocks_ref[k] * vec[:, k : k + 1], axis=0, keepdims=True)
            out = out + jnp.where(cb_at == cols[k], prod, 0.0)
        return out

    part_buf[row] = backward(y_ref)
    arrive = send(3, [row_device(d) for d in line_r], part_buf, row)
    hot_at = lax.broadcasted_iota(jnp.int32, (2 * rb, LANES), 0).astype(jnp.float32)
    for g in range(nq // qper):
        code = total([max_q[i, rb : rb + 1] for i in range(g * qper, (g + 1) * qper)], jnp.add)
        hot_ref[:, g * LANES : (g + 1) * LANES] = jnp.where(hot_at == code, 1.0, 0.0).astype(jnp.bfloat16)
    rhs_s = row_scale * rhs_ref[...]
    arrive()
    grad = cost_s - whole(part_buf, jnp.add) * col_scale
    x_new = jnp.clip(x_prev - tau * grad, 0.0, upper_s)
    delta_x = x_new - x_prev
    vec_ref[0] = x_new * col_scale
    vec_ref[1] = delta_x * col_scale

    vecs = stacked([vec_ref[v, pl.ds(bcol[k], 1), :] for v in range(2) for k in range(nbd)]).T
    fwd_buf[slot] = stacked(
        [
            jnp.sum(flip_ref[k] * vecs[:, v * nbd + k : v * nbd + k + 1], axis=0, keepdims=True)
            for v in range(2)
            for k in range(nbd)
        ]
    )
    arrive = send(4, [col_device(d) for d in everyone], fwd_buf, slot)
    x_out[...] = x_new
    arrive()
    rest = fwd_buf[...].reshape(ncol * 2 * nbd, LANES)
    hot = hot_ref[...]
    pair = jnp.zeros((2 * rb, LANES), jnp.float32)
    for _ in range(3):
        part = rest.astype(jnp.bfloat16)
        rest = rest - part.astype(jnp.float32)
        pair = pair + jnp.dot(hot, part, preferred_element_type=jnp.float32)
    ax = pair[:rb] * row_scale
    adx = pair[rb:] * row_scale
    y_prev = y_ref[...]
    y_new = y_prev + sigma * (rhs_s - ax - adx)
    y_out[...] = y_new
    back_buf[row] = backward(y_out)
    arrive = send(5, [row_device(d) for d in line_r], back_buf, row)
    delta_y = y_new - y_prev
    resid = rhs_s - ax
    for at, term in enumerate((delta_y * delta_y, adx * adx, resid * resid, rhs_s * y_new)):
        dual_buf[row, at : at + 1] = jnp.sum(term, axis=0, keepdims=True)
    arrive_dual = send(6, [row_device(d) for d in line_r], dual_buf, row)

    def folded(term):
        out = jnp.sum(term, axis=0, keepdims=True)
        return out + pltpu.roll(out, LANES // 2, 1)

    moved = folded(delta_x * delta_x)
    left = lax.broadcasted_iota(jnp.int32, (1, LANES), 1) < LANES // 2
    arrive()
    reduced = cost_s - whole(back_buf, jnp.add) * col_scale
    sum_buf[slot] = jnp.where(left, moved, folded(cost_s * x_new + upper_s * jnp.maximum(-reduced, 0.0)))
    arrive = send(7, [mirror_device(d) for d in everyone], sum_buf, slot)
    arrive_dual()
    dual = jnp.sum(whole(dual_buf, jnp.add), axis=1, keepdims=True)
    dy2, adx2, res2, by = dual[0:1], dual[1:2], dual[2:3], dual[3:4]
    m = rb * LANES * nrow
    n = cb * LANES * ncol
    for copy in finish[:-1]:
        copy.wait()
    arrive()
    primal = whole(sum_buf, jnp.add)
    dx2 = jnp.sum(jnp.where(left, primal, 0.0), axis=1, keepdims=True)
    gain = jnp.sum(jnp.where(left, 0.0, primal), axis=1, keepdims=True)
    movement = 0.5 * omega * dx2 + 0.5 / omega_v * dy2
    at = lax.broadcasted_iota(jnp.int32, (1, LANES), 1)
    stats_out[...] = jnp.where(
        at == 0,
        jnp.sqrt(res2 / m),
        jnp.where(at == 1, (gain - by) / n, movement / jnp.sqrt(adx2 * dy2 + 1e-06)),
    )
    finish[-1].wait()


def shards(grid, nrow, blocks, block_rows, block_cols, counts, x_prev, y_prev, cost, rhs, upper, steps):
    nx, ny, nz = grid
    nbd, bsz = blocks.shape[2], blocks.shape[3]
    rb = y_prev.shape[0] // bsz
    cb = x_prev.shape[0] // bsz
    ncol = nx * ny * nz
    vmem = pl.BlockSpec(memory_space=pltpu.VMEM)
    hbm = pl.BlockSpec(memory_space=pl.ANY)
    f32 = jnp.float32

    def buf(*shape):
        return pltpu.VMEM((*shape, LANES), f32)

    x_new, y_new, stats = pl.pallas_call(
        functools.partial(body, grid, nrow, nbd),
        out_shape=(
            jax.ShapeDtypeStruct((cb, bsz), f32),
            jax.ShapeDtypeStruct((rb, bsz), f32),
            jax.ShapeDtypeStruct((1, LANES), f32),
        ),
        in_specs=[hbm] * 10,
        out_specs=(vmem, vmem, vmem),
        scratch_shapes=[
            pltpu.SMEM((1, 1, nbd), jnp.int32), pltpu.SMEM((1, 1, nbd), jnp.int32),
            pltpu.SMEM((1, 1), jnp.int32), pltpu.SMEM((2,), f32),
            buf(nbd, bsz), buf(cb), buf(rb), buf(cb), buf(rb), buf(cb),
            buf(nbd, bsz), buf(2, cb), buf(rb), pltpu.VMEM((2 * rb, ncol * 2 * nbd), jnp.bfloat16),
            buf(ny, 2 * nbd), buf(nx * nz, rb + 8), buf(nrow, cb), buf(nrow, cb), buf(ncol, 2 * nbd),
            buf(nrow, 4), buf(nrow, cb), buf(ncol, 1),
            pltpu.SemaphoreType.DMA((10,)),
            pltpu.SemaphoreType.DMA((8,)),
            pltpu.SemaphoreType.DMA((8,)),
            pltpu.SemaphoreType.REGULAR,
        ],
        compiler_params=pltpu.CompilerParams(collective_id=0, has_side_effects=True),
        name="pdlp",
    )(
        block_rows,
        block_cols,
        counts,
        steps,
        blocks.reshape(nbd, bsz, bsz),
        x_prev.reshape(cb, bsz),
        y_prev.reshape(rb, bsz),
        cost.reshape(cb, bsz),
        rhs.reshape(rb, bsz),
        upper.reshape(cb, bsz),
    )
    return x_new.reshape(-1), y_new.reshape(-1), stats[0, :3]


def solution(mesh):
    placed = (
        P("row", "col", None, None, None),
        P("row", "col", None),
        P("row", "col", None),
        P("row", "col"),
        P("col"),
        P("row"),
        P("col"),
        P("row"),
        P("col"),
        P(),
    )
    return jax.shard_map(
        functools.partial(shards, COL_GRID[mesh.shape["col"]], mesh.shape["row"]),
        mesh=mesh,
        in_specs=placed,
        out_specs=(P("col"), P("row"), P()),
        check_vma=False,
    )
```

```python
import functools

import jax
import jax.numpy as jnp
from jax import lax
from jax.experimental import pallas as pl
from jax.experimental.pallas import tpu as pltpu
from jax.sharding import PartitionSpec as P

MESH = pl.DeviceIdType.MESH
LANES = 128
NOWHERE = 1000.0
COL_GRID = {128: (2, 8, 8), 16: (2, 4, 2)}


def hops(d, n):
    return min(d, n - d)


def far_first(n):
    return sorted(range(1, n), key=lambda d: -hops(d, n))


def total(terms, op):
    acc = terms[0]
    for term in terms[1:]:
        acc = op(acc, term)
    return acc


def body(
    grid, nrow, nbd,
    brow_hbm, bcol_hbm, count_ref, steps_hbm, blocks_hbm, x_hbm, y_hbm, cost_hbm, rhs_hbm, upper_hbm,
    x_out, y_out, stats_out,
    brow_ref, bcol_ref, steps_ref, blocks_ref, x_ref, y_ref, cost_ref, rhs_ref, upper_ref,
    flip_ref, vec_ref, scale_ref, hot_ref,
    max_y, max_q, cmax_buf, part_buf, fwd_buf, move_buf, half_buf, term_buf, dual_buf, back_buf, sum_buf,
    local_sems, send_sems, recv_sems, reached,
):
    nx, ny, nz = grid
    rb = y_ref.shape[0]
    cb = x_ref.shape[0]
    nq = nx * nz
    ncol = nq * ny
    qlanes = ny * nbd
    qper = min(LANES // qlanes, nq)
    row = lax.axis_index("row")
    col = lax.axis_index("col")
    xh = lax.div(col, ny * nz)
    yi = lax.rem(lax.div(col, nz), ny)
    zi = lax.rem(col, nz)
    xs = [lax.rem(xh + d, nx) for d in range(nx)]
    ys = [lax.rem(yi + d, ny) for d in range(ny)]
    zs = [lax.rem(zi + d, nz) for d in range(nz)]
    rs = [lax.rem(row + d, nrow) for d in range(nrow)]
    qi = xh * nz + zi
    slot = qi * ny + yi

    def col_device(d):
        dx, dy, dz = d
        return (row, (xs[dx] * ny + ys[dy]) * nz + zs[dz])

    def row_device(d):
        return (rs[d], col)

    def ring_device(d):
        return (rs[d[1]], col_device((d[0], 0, 0))[1])

    def ordered(offsets):
        cost = lambda d: (nx // 2) * 4 * d[0] + hops(d[1], ny) + hops(d[2], nz)
        return sorted(offsets, key=lambda d: -cost(d))

    line_y = [(0, d, 0) for d in far_first(ny)]
    line_z = [(0, 0, d) for d in far_first(nz)]
    plane = ordered([(a, 0, c) for a in range(nx) for c in range(nz) if a or c])
    everyone = ordered([(a, b, c) for a in range(nx) for b in range(ny) for c in range(nz) if a or b or c])
    sheet = [d for d in everyone if not d[0]]
    line_r = far_first(nrow)
    ring = [(a, d) for a in range(nx - 1, -1, -1) for d in far_first(nrow) + [0] * a]
    partner = [col_device((1, 0, 0))]

    barrier = pltpu.get_barrier_semaphore()
    near = [col_device(d) for d in line_y] + [row_device(d) for d in line_r]
    near += [col_device(d) for d in line_z] + [col_device((1, 0, 0))]
    fetches = [
        pltpu.make_async_copy(src, dst, local_sems.at[i])
        for i, (src, dst) in enumerate(
            (
                (blocks_hbm, blocks_ref), (brow_hbm, brow_ref), (bcol_hbm, bcol_ref),
                (y_hbm, y_ref), (x_hbm, x_ref), (cost_hbm, cost_ref), (rhs_hbm, rhs_ref), (upper_hbm, upper_ref),
                (steps_hbm, steps_ref),
            )
        )
    ]
    for copy in fetches:
        copy.start()
    for device in near:
        pl.semaphore_signal(barrier, inc=1, device_id=device, device_id_type=MESH)
    finish = []

    def send(at, peers, buf, me):
        for device in peers:
            pltpu.make_async_remote_copy(
                src_ref=buf.at[me],
                dst_ref=buf.at[me],
                send_sem=send_sems.at[at],
                recv_sem=recv_sems.at[at],
                device_id=device,
                device_id_type=MESH,
            ).start()
        theirs = buf.at[pl.ds(0, len(peers))]
        finish.append(pltpu.make_async_copy(theirs, theirs, send_sems.at[at]))
        return pltpu.make_async_copy(theirs, theirs, recv_sems.at[at]).wait

    def whole(buf, op):
        return total([buf[i] for i in range(buf.shape[0])], op)

    for copy in fetches[:3]:
        copy.wait()
    count = count_ref[0, 0]
    brow = [brow_ref[0, 0, k] for k in range(nbd)]
    bcol = [bcol_ref[0, 0, k] for k in range(nbd)]
    rows = [jnp.where(k < count, brow[k].astype(jnp.float32), NOWHERE) for k in range(nbd)]
    cols = [jnp.where(k < count, bcol[k], -1) for k in range(nbd)]
    tile_at = lax.broadcasted_iota(jnp.int32, (2 * nbd, LANES), 0)
    cb_at = lax.broadcasted_iota(jnp.int32, (cb, LANES), 0)

    def stacked(entries):
        out = jnp.zeros((len(entries), LANES), jnp.float32)
        for i, entry in enumerate(entries):
            out = jnp.where(tile_at == i, entry, out)
        return out

    col_peak = jnp.zeros((cb, LANES), jnp.float32)
    row_peaks = []
    for k in range(nbd):
        block = blocks_ref[k]
        flip = block.T
        flip_ref[k] = flip
        row_peaks.append(jnp.max(jnp.abs(flip), axis=0, keepdims=True))
        peak = jnp.max(jnp.abs(block), axis=0, keepdims=True)
        col_peak = jnp.maximum(col_peak, jnp.where(cb_at == cols[k], peak, 0.0))
    max_y[yi] = stacked(row_peaks + rows)
    cmax_buf[row] = col_peak
    pl.semaphore_wait(barrier, len(near))
    pl.semaphore_signal(reached, inc=1, device_id=col_device((1, 0, 0)), device_id_type=MESH)
    arrive = send(0, [col_device(d) for d in line_y], max_y, yi)
    arrive_c = send(1, [row_device(d) for d in line_r], cmax_buf, row)
    for copy in fetches[3:]:
        copy.wait()
    arrive()

    rb_at = lax.broadcasted_iota(jnp.int32, (rb, LANES), 0).astype(jnp.float32)
    lane = lax.broadcasted_iota(jnp.int32, (2 * nbd, LANES), 1)
    mine = (lane // qlanes == lax.rem(qi, qper)) & (tile_at - nbd == lane % nbd)
    owner = lane % qlanes // nbd
    dense = jnp.zeros((rb, LANES), jnp.float32)
    codes = jnp.zeros((2 * nbd, LANES), jnp.float32)
    for j in range(ny):
        for k in range(nbd):
            here = rb_at == max_y[j, nbd + k : nbd + k + 1]
            dense = jnp.maximum(dense, jnp.where(here, max_y[j, k : k + 1], 0.0))
        codes = jnp.where(mine & (owner == j), max_y[j], codes)
    max_q[qi, :rb] = dense
    max_q[qi, rb:] = jnp.broadcast_to(jnp.sum(codes, axis=0, keepdims=True), (8, LANES))
    pl.semaphore_wait(reached, 1)
    arrive = send(2, [col_device(d) for d in plane], max_q, qi)
    arrive_c()
    col_scale = 1.0 / jnp.sqrt(jnp.maximum(whole(cmax_buf, jnp.maximum), 0.5))
    cost_s = col_scale * cost_ref[...]
    upper_s = upper_ref[...] / col_scale
    x_prev = x_ref[...]
    eta = steps_ref[0]
    omega = steps_ref[1]
    omega_v = jnp.full((1, 1), omega)
    tau = eta / omega_v
    sigma = eta * omega
    arrive()
    rowmax = total([max_q[i, :rb] for i in range(nq)], jnp.maximum)
    row_scale = 1.0 / jnp.sqrt(jnp.maximum(rowmax, 0.5))
    scale_ref[...] = row_scale

    def backward(ref):
        got = [ref[pl.ds(brow[k], 1), :] * scale_ref[pl.ds(brow[k], 1), :] for k in range(nbd)]
        vec = stacked(got + got).T
        out = jnp.zeros((cb, LANES), jnp.float32)
        for k in range(nbd):
            prod = jnp.sum(blocks_ref[k] * vec[:, k : k + 1], axis=0, keepdims=True)
            out = out + jnp.where(cb_at == cols[k], prod, 0.0)
        return out

    part_buf[row] = backward(y_ref)
    arrive = send(3, [row_device(d) for d in line_r], part_buf, row)
    half_buf[xh, :cb] = cost_s
    half_buf[xh, cb : 2 * cb] = upper_s
    half_buf[xh, 2 * cb :] = col_scale
    arrive_half = send(4, partner, half_buf, xh)
    for g in range(nq // qper):
        code = total([max_q[i, rb : rb + 1] for i in range(g * qper, (g + 1) * qper)], jnp.add)
        hot_ref[:, g * LANES : (g + 1) * LANES] = jnp.where(rb_at == code, 1.0, 0.0).astype(jnp.bfloat16)
    rhs_s = row_scale * rhs_ref[...]
    arrive()
    grad = cost_s - whole(part_buf, jnp.add) * col_scale
    x_new = jnp.clip(x_prev - tau * grad, 0.0, upper_s)
    delta_x = x_new - x_prev
    vec_ref[0] = (x_new + delta_x) * col_scale
    vec_ref[1] = delta_x * col_scale

    vecs = stacked([vec_ref[v, pl.ds(bcol[k], 1), :] for v in range(2) for k in range(nbd)]).T

    def forward(v):
        prods = [
            jnp.sum(flip_ref[k] * vecs[:, v * nbd + k : v * nbd + k + 1], axis=0, keepdims=True) for k in range(nbd)
        ]
        return stacked(prods + prods)[:nbd]

    def gathered(ref):
        rest = ref[...].reshape(ncol * nbd, LANES)
        hot = hot_ref[:, : ncol * nbd]
        out = jnp.zeros((rb, LANES), jnp.float32)
        for _ in range(3):
            part = rest.astype(jnp.bfloat16)
            rest = rest - part.astype(jnp.float32)
            out = out + jnp.dot(hot, part, preferred_element_type=jnp.float32)
        return out * row_scale

    def folded(term):
        out = jnp.sum(term, axis=0, keepdims=True)
        return out + pltpu.roll(out, LANES // 2, 1)

    fwd_buf[slot] = forward(0)
    arrive = send(5, [col_device(d) for d in everyone], fwd_buf, slot)
    move_buf[slot] = forward(1)
    arrive_move = send(6, [col_device(d) for d in everyone], move_buf, slot)
    left = lax.broadcasted_iota(jnp.int32, (1, LANES), 1) < LANES // 2
    term_buf[xh] = jnp.where(left, folded(delta_x * delta_x), folded(cost_s * x_new))
    arrive_term = send(7, partner, term_buf, xh)
    x_out[...] = x_new
    y_prev = y_ref[...]
    arrive()
    both = gathered(fwd_buf)
    y_new = y_prev + sigma * (rhs_s - both)
    y_out[...] = y_new
    mine_at = xh * nrow + row
    back_buf[mine_at] = backward(y_out)
    arrive = send(8, [ring_device(d) for d in ring], back_buf, mine_at)
    arrive_half()
    arrive_term()
    terms = total([term_buf[h] for h in range(nx)], jnp.add)
    arrive()
    gains = []
    for h in range(nx):
        product = total([back_buf[h * nrow + r] for r in range(nrow)], jnp.add)
        reduced = half_buf[h, :cb] - product * half_buf[h, 2 * cb :]
        gains.append(folded(half_buf[h, cb : 2 * cb] * jnp.maximum(-reduced, 0.0)))
    spot = yi * nz + zi
    sum_buf[spot] = terms + jnp.where(left, 0.0, total(gains, jnp.add))
    arrive = send(9, [col_device(d) for d in sheet], sum_buf, spot)
    arrive_move()
    adx = gathered(move_buf)
    delta_y = y_new - y_prev
    resid = rhs_s - (both - adx)
    for at, term in enumerate((delta_y * delta_y, adx * adx, resid * resid, rhs_s * y_new)):
        dual_buf[row, at : at + 1] = jnp.sum(term, axis=0, keepdims=True)
    arrive_dual = send(10, [row_device(d) for d in line_r], dual_buf, row)
    for copy in finish[:-2]:
        copy.wait()
    arrive_dual()
    dual = jnp.sum(whole(dual_buf, jnp.add), axis=1, keepdims=True)
    dy2, adx2, res2, by = dual[0:1], dual[1:2], dual[2:3], dual[3:4]
    m = rb * LANES * nrow
    n = cb * LANES * ncol
    arrive()
    primal = whole(sum_buf, jnp.add)
    dx2 = jnp.sum(jnp.where(left, primal, 0.0), axis=1, keepdims=True)
    gain = jnp.sum(jnp.where(left, 0.0, primal), axis=1, keepdims=True)
    movement = 0.5 * omega * dx2 + 0.5 / omega_v * dy2
    at = lax.broadcasted_iota(jnp.int32, (1, LANES), 1)
    stats_out[...] = jnp.where(
        at == 0,
        jnp.sqrt(res2 / m),
        jnp.where(at == 1, (gain - by) / n, movement / jnp.sqrt(adx2 * dy2 + 1e-06)),
    )
    for copy in finish[-2:]:
        copy.wait()


def publish(x_ref, y_ref, stats_ref, x_out, y_out, stats_out):
    x_out[...] = x_ref[...]
    y_out[...] = y_ref[...]
    stats_out[...] = stats_ref[:, :3]


def shards(grid, nrow, blocks, block_rows, block_cols, counts, x_prev, y_prev, cost, rhs, upper, steps):
    nx, ny, nz = grid
    nbd, bsz = blocks.shape[2], blocks.shape[3]
    rb = y_prev.shape[0] // bsz
    cb = x_prev.shape[0] // bsz
    ncol = nx * ny * nz
    vmem = pl.BlockSpec(memory_space=pltpu.VMEM)
    hbm = pl.BlockSpec(memory_space=pltpu.HBM)
    f32 = jnp.float32

    def buf(*shape):
        return pltpu.VMEM((*shape, LANES), f32)

    x_new, y_new, stats = pl.pallas_call(
        functools.partial(body, grid, nrow, nbd),
        out_shape=(
            pltpu.VMEM((cb, bsz), f32),
            pltpu.VMEM((rb, bsz), f32),
            pltpu.VMEM((1, LANES), f32),
        ),
        in_specs=[hbm] * 2 + [pl.BlockSpec(memory_space=pltpu.SMEM)] + [hbm] * 7,
        out_specs=(vmem, vmem, vmem),
        scratch_shapes=[
            pltpu.SMEM((1, 1, nbd), jnp.int32), pltpu.SMEM((1, 1, nbd), jnp.int32),
            pltpu.SMEM((2,), f32),
            buf(nbd, bsz), buf(cb), buf(rb), buf(cb), buf(rb), buf(cb),
            buf(nbd, bsz), buf(2, cb), buf(rb), pltpu.VMEM((rb, max(ncol * nbd, LANES)), jnp.bfloat16),
            buf(ny, 2 * nbd), buf(nx * nz, rb + 8), buf(nrow, cb), buf(nrow, cb), buf(ncol, nbd), buf(ncol, nbd),
            buf(nx, 3 * cb), buf(nx, 1), buf(nrow, 4), buf(nx * nrow, cb), buf(ny * nz, 1),
            pltpu.SemaphoreType.DMA((9,)),
            pltpu.SemaphoreType.DMA((11,)),
            pltpu.SemaphoreType.DMA((11,)),
            pltpu.SemaphoreType.REGULAR,
        ],
        compiler_params=pltpu.CompilerParams(collective_id=0, has_side_effects=True),
        name="pdlp",
    )(
        block_rows,
        block_cols,
        counts,
        steps,
        blocks.reshape(nbd, bsz, bsz),
        x_prev.reshape(cb, bsz),
        y_prev.reshape(rb, bsz),
        cost.reshape(cb, bsz),
        rhs.reshape(rb, bsz),
        upper.reshape(cb, bsz),
    )
    x_new, y_new, stats = pl.pallas_call(
        publish,
        out_shape=(
            jax.ShapeDtypeStruct((cb, bsz), f32),
            jax.ShapeDtypeStruct((rb, bsz), f32),
            jax.ShapeDtypeStruct((1, 3), f32),
        ),
        in_specs=[vmem] * 3,
        out_specs=(vmem,) * 3,
        name="publish",
    )(*(pltpu.with_memory_space_constraint(a, pltpu.VMEM) for a in (x_new, y_new, stats)))
    return x_new.reshape(-1), y_new.reshape(-1), stats.reshape(-1)


def solution(mesh):
    placed = (
        P("row", "col", None, None, None),
        P("row", "col", None),
        P("row", "col", None),
        P("row", "col"),
        P("col"),
        P("row"),
        P("col"),
        P("row"),
        P("col"),
        P(),
    )
    return jax.shard_map(
        functools.partial(shards, COL_GRID[mesh.shape["col"]], mesh.shape["row"]),
        mesh=mesh,
        in_specs=placed,
        out_specs=(P("col"), P("row"), P()),
        check_vma=False,
    )
```

```python
import functools

import jax
import jax.numpy as jnp
from jax import lax
from jax.experimental import pallas as pl
from jax.experimental.pallas import tpu as pltpu
from jax.sharding import PartitionSpec as P

MESH = pl.DeviceIdType.MESH
LANES = 128
NOWHERE = 1000.0
COL_GRID = {128: (2, 8, 8), 16: (2, 4, 2)}


def hops(d, n):
    return min(d, n - d)


def far_first(n):
    return sorted(range(1, n), key=lambda d: -hops(d, n))


def total(terms, op):
    acc = terms[0]
    for term in terms[1:]:
        acc = op(acc, term)
    return acc


def body(
    grid, nrow, nbd,
    brow_hbm, bcol_hbm, count_ref, steps_hbm, blocks_hbm, x_hbm, y_hbm, cost_hbm, rhs_hbm, upper_hbm,
    x_out, y_out, stats_out,
    brow_ref, bcol_ref, steps_ref, blocks_ref, x_ref, y_ref, cost_ref, rhs_ref, upper_ref,
    flip_ref, vec_ref, scale_ref, hot_ref,
    max_y, max_q, code_q, cmax_buf, part_buf, fwd_buf, both_ref, move_send, move_y, move_q, half_buf, term_buf,
    dual_buf, back_buf, sum_buf,
    local_sems, send_sems, recv_sems, reached,
):
    nx, ny, nz = grid
    rb = y_ref.shape[0]
    cb = x_ref.shape[0]
    nq = nx * nz
    ncol = nq * ny
    qlanes = ny * nbd
    qper = min(LANES // qlanes, nz)
    width = qper * qlanes
    half = ny * nz
    share = rb // ny
    row = lax.axis_index("row")
    col = lax.axis_index("col")
    xh = lax.div(col, ny * nz)
    yi = lax.rem(lax.div(col, nz), ny)
    zi = lax.rem(col, nz)
    xs = [lax.rem(xh + d, nx) for d in range(nx)]
    ys = [lax.rem(yi + d, ny) for d in range(ny)]
    zs = [lax.rem(zi + d, nz) for d in range(nz)]
    rs = [lax.rem(row + d, nrow) for d in range(nrow)]
    qi = xh * nz + zi
    slot = qi * ny + yi

    def col_device(d):
        dx, dy, dz = d
        return (row, (xs[dx] * ny + ys[dy]) * nz + zs[dz])

    def row_device(d):
        return (rs[d], col)

    def table_device(d):
        return (rs[d[1]], col_device((0, d[0], 0))[1])

    def ring_device(d):
        return (rs[d[1]], col_device((d[0], 0, 0))[1])

    def ordered(offsets):
        cost = lambda d: (nx // 2) * 4 * d[0] + hops(d[1], ny) + hops(d[2], nz)
        return sorted(offsets, key=lambda d: -cost(d))

    line_y = [(0, d, 0) for d in far_first(ny)]
    line_z = [(0, 0, d) for d in far_first(nz)]
    plane = ordered([(a, 0, c) for a in range(nx) for c in range(nz) if a or c])
    everyone = ordered([(a, b, c) for a in range(nx) for b in range(ny) for c in range(nz) if a or b or c])
    sheet = [d for d in everyone if not d[0]]
    beyond = [d for d in everyone if d[0]]
    line_r = far_first(nrow)
    ring = [(a, d) for a in range(nx - 1, -1, -1) for d in far_first(nrow) + [0] * a]
    partner = [col_device((1, 0, 0))]
    table = [(b, d) for b in far_first(ny) + [0] for d in far_first(nrow) + [0] if b or d]

    barrier = pltpu.get_barrier_semaphore()
    near = [col_device(d) for d in line_y] + [row_device(d) for d in line_r]
    near += [col_device(d) for d in line_z] + [col_device((1, 0, 0))]
    fetches = [
        pltpu.make_async_copy(src, dst, local_sems.at[i])
        for i, (src, dst) in enumerate(
            (
                (blocks_hbm, blocks_ref), (brow_hbm, brow_ref), (bcol_hbm, bcol_ref),
                (y_hbm, y_ref), (x_hbm, x_ref), (cost_hbm, cost_ref), (rhs_hbm, rhs_ref), (upper_hbm, upper_ref),
                (steps_hbm, steps_ref),
            )
        )
    ]
    for copy in fetches:
        copy.start()
    for device in near:
        pl.semaphore_signal(barrier, inc=1, device_id=device, device_id_type=MESH)
    finish = []

    def send(at, peers, buf, me, sources=None):
        for i, device in enumerate(peers):
            pltpu.make_async_remote_copy(
                src_ref=sources[i] if sources else buf.at[me],
                dst_ref=buf.at[me],
                send_sem=send_sems.at[at],
                recv_sem=recv_sems.at[at],
                device_id=device,
                device_id_type=MESH,
            ).start()
        theirs = buf.at[pl.ds(0, len(peers))]
        finish.append(pltpu.make_async_copy(theirs, theirs, send_sems.at[at]))
        return pltpu.make_async_copy(theirs, theirs, recv_sems.at[at]).wait

    def whole(buf, op):
        return total([buf[i] for i in range(buf.shape[0])], op)

    for copy in fetches[:3]:
        copy.wait()
    count = count_ref[0, 0]
    brow = [brow_ref[0, 0, k] for k in range(nbd)]
    bcol = [bcol_ref[0, 0, k] for k in range(nbd)]
    rows = [jnp.where(k < count, brow[k].astype(jnp.float32), NOWHERE) for k in range(nbd)]
    cols = [jnp.where(k < count, bcol[k], -1) for k in range(nbd)]
    tile_at = lax.broadcasted_iota(jnp.int32, (2 * nbd, LANES), 0)
    cb_at = lax.broadcasted_iota(jnp.int32, (cb, LANES), 0)

    def stacked(entries):
        out = jnp.zeros((len(entries), LANES), jnp.float32)
        for i, entry in enumerate(entries):
            out = jnp.where(tile_at == i, entry, out)
        return out

    col_peak = jnp.zeros((cb, LANES), jnp.float32)
    row_peaks = []
    for k in range(nbd):
        block = blocks_ref[k]
        flip = block.T
        flip_ref[k] = flip
        row_peaks.append(jnp.max(jnp.abs(flip), axis=0, keepdims=True))
        peak = jnp.max(jnp.abs(block), axis=0, keepdims=True)
        col_peak = jnp.maximum(col_peak, jnp.where(cb_at == cols[k], peak, 0.0))
    max_y[yi] = stacked(row_peaks + rows)
    cmax_buf[row] = col_peak
    pl.semaphore_wait(barrier, len(near))
    pl.semaphore_signal(reached, inc=1, device_id=col_device((1, 0, 0)), device_id_type=MESH)
    arrive = send(0, [col_device(d) for d in line_y], max_y, yi)
    arrive_c = send(1, [row_device(d) for d in line_r], cmax_buf, row)
    for copy in fetches[3:]:
        copy.wait()
    rb_at = lax.broadcasted_iota(jnp.int32, (rb, LANES), 0).astype(jnp.float32)
    lane = lax.broadcasted_iota(jnp.int32, (2 * nbd, LANES), 1)
    mine = (lane // qlanes == lax.rem(qi, qper)) & (tile_at - nbd == lane % nbd)
    owner = lane % qlanes // nbd
    arrive()
    dense = jnp.zeros((rb, LANES), jnp.float32)
    for j in range(ny):
        for k in range(nbd):
            here = rb_at == max_y[j, nbd + k : nbd + k + 1]
            dense = jnp.maximum(dense, jnp.where(here, max_y[j, k : k + 1], 0.0))
    max_q[qi] = dense
    pl.semaphore_wait(reached, 1)
    arrive = send(2, [col_device(d) for d in plane], max_q, qi)
    codes = jnp.zeros((2 * nbd, LANES), jnp.float32)
    for j in range(ny):
        codes = jnp.where(mine & (owner == j), max_y[j], codes)
    code_q[qi] = jnp.sum(codes, axis=0, keepdims=True)
    arrive_code = send(3, [col_device(d) for d in plane], code_q, qi)
    arrive_c()
    col_scale = 1.0 / jnp.sqrt(jnp.maximum(whole(cmax_buf, jnp.maximum), 0.5))
    cost_s = col_scale * cost_ref[...]
    upper_s = upper_ref[...] / col_scale
    x_prev = x_ref[...]
    eta = steps_ref[0]
    omega = steps_ref[1]
    omega_v = jnp.full((1, 1), omega)
    tau = eta / omega_v
    sigma = eta * omega
    arrive()
    rowmax = whole(max_q, jnp.maximum)
    row_scale = 1.0 / jnp.sqrt(jnp.maximum(rowmax, 0.5))
    scale_ref[...] = row_scale

    def backward(ref):
        got = [ref[pl.ds(brow[k], 1), :] * scale_ref[pl.ds(brow[k], 1), :] for k in range(nbd)]
        vec = stacked(got + got).T
        out = jnp.zeros((cb, LANES), jnp.float32)
        for k in range(nbd):
            prod = jnp.sum(blocks_ref[k] * vec[:, k : k + 1], axis=0, keepdims=True)
            out = out + jnp.where(cb_at == cols[k], prod, 0.0)
        return out

    part_buf[row] = backward(y_ref)
    arrive = send(12, [row_device(d) for d in line_r], part_buf, row)
    half_buf[xh, :cb] = cost_s
    half_buf[xh, cb : 2 * cb] = upper_s
    half_buf[xh, 2 * cb :] = col_scale
    arrive_half = send(4, partner, half_buf, xh)
    arrive_code()
    for g in range(nq // qper):
        code = total([code_q[i] for i in range(g * qper, (g + 1) * qper)], jnp.add)
        h, start = divmod(g * width, half * nbd)
        hot_ref[h, :, start : start + width] = jnp.where(rb_at == code, 1.0, 0.0).astype(jnp.bfloat16)[:, :width]
    rhs_s = row_scale * rhs_ref[...]
    arrive()
    grad = cost_s - whole(part_buf, jnp.add) * col_scale
    x_new = jnp.clip(x_prev - tau * grad, 0.0, upper_s)
    delta_x = x_new - x_prev
    vec_ref[0] = (x_new + delta_x) * col_scale
    vec_ref[1] = delta_x * col_scale

    vecs = stacked([vec_ref[v, pl.ds(bcol[k], 1), :] for v in range(2) for k in range(nbd)]).T

    def forward(v):
        return [
            jnp.sum(flip_ref[k] * vecs[:, v * nbd + k : v * nbd + k + 1], axis=0, keepdims=True) for k in range(nbd)
        ]

    def gathered(ref, h):
        rest = ref[pl.ds(h * half, half)].reshape(half * nbd, LANES)
        hot = hot_ref[h]
        out = jnp.zeros((rb, LANES), jnp.float32)
        for _ in range(3):
            part = rest.astype(jnp.bfloat16)
            rest = rest - part.astype(jnp.float32)
            out = out + jnp.dot(hot, part, preferred_element_type=jnp.float32)
        return out

    def folded(term):
        out = jnp.sum(term, axis=0, keepdims=True)
        return out + pltpu.roll(out, LANES // 2, 1)

    prods = forward(0)
    fwd_buf[slot] = stacked(prods + prods)[:nbd]
    arrive_far = send(5, [col_device(d) for d in beyond], fwd_buf, slot)
    prods = forward(1)
    share_at = lax.broadcasted_iota(jnp.int32, (share, LANES), 0).astype(jnp.float32)
    for j in range(ny):
        move_send[j] = total([jnp.where(share_at + j * share == rows[k], prods[k], 0.0) for k in range(nbd)], jnp.add)
    move_y[yi] = move_send[yi]
    arrive_move = send(6, [col_device(d) for d in line_y], move_y, yi, [move_send.at[ys[d[1]]] for d in line_y])
    arrive = send(11, [col_device(d) for d in sheet], fwd_buf, slot)
    left = lax.broadcasted_iota(jnp.int32, (1, LANES), 1) < LANES // 2
    term_buf[xh] = jnp.where(left, folded(delta_x * delta_x), folded(cost_s * x_new))
    arrive_term = send(7, partner, term_buf, xh)
    x_out[...] = x_new
    y_prev = y_ref[...]
    arrive_move()
    move_q[qi] = whole(move_y, jnp.add)
    arrive_move = send(13, [col_device(d) for d in plane], move_q, qi)
    arrive()
    both = gathered(fwd_buf, xh)
    arrive_far()
    both = (both + gathered(fwd_buf, 1 - xh)) * row_scale
    both_ref[...] = rhs_s - both
    y_new = y_prev + sigma * (rhs_s - both)
    y_out[...] = y_new
    mine_at = xh * nrow + row
    back_buf[mine_at] = backward(y_out)
    arrive = send(8, [ring_device(d) for d in ring], back_buf, mine_at)
    arrive_move()
    at = pl.ds(pl.multiple_of(yi * share, share), share)
    scale = scale_ref[at, :]
    adx = whole(move_q, jnp.add) * scale
    y_share = y_out[at, :]
    delta_y = y_share - y_ref[at, :]
    resid = both_ref[at, :] + adx
    quarter = lax.broadcasted_iota(jnp.int32, (1, LANES), 1) // (LANES // 4)
    duals = jnp.zeros((1, LANES), jnp.float32)
    for i, term in enumerate((delta_y * delta_y, adx * adx, resid * resid, scale * rhs_ref[at, :] * y_share)):
        term = folded(term)
        duals = jnp.where(quarter == i, term + pltpu.roll(term, LANES // 4, 1), duals)
    spot = yi * nrow + row
    dual_buf[spot] = duals
    arrive_dual = send(10, [table_device(d) for d in table], dual_buf, spot)
    arrive_half()
    arrive_term()
    terms = total([term_buf[h] for h in range(nx)], jnp.add)
    arrive()
    gains = []
    for h in range(nx):
        product = total([back_buf[h * nrow + r] for r in range(nrow)], jnp.add)
        reduced = half_buf[h, :cb] - product * half_buf[h, 2 * cb :]
        gains.append(folded(half_buf[h, cb : 2 * cb] * jnp.maximum(-reduced, 0.0)))
    spot = yi * nz + zi
    sum_buf[spot] = terms + jnp.where(left, 0.0, total(gains, jnp.add))
    arrive = send(9, [col_device(d) for d in sheet], sum_buf, spot)
    for copy in finish[:-1]:
        copy.wait()
    arrive_dual()
    dual = whole(dual_buf, jnp.add)
    dy2, adx2, res2, by = (jnp.sum(jnp.where(quarter == i, dual, 0.0), axis=1, keepdims=True) for i in range(4))
    m = rb * LANES * nrow
    n = cb * LANES * ncol
    arrive()
    primal = whole(sum_buf, jnp.add)
    dx2 = jnp.sum(jnp.where(left, primal, 0.0), axis=1, keepdims=True)
    gain = jnp.sum(jnp.where(left, 0.0, primal), axis=1, keepdims=True)
    movement = 0.5 * omega * dx2 + 0.5 / omega_v * dy2
    at = lax.broadcasted_iota(jnp.int32, (1, LANES), 1)
    stats_out[...] = jnp.where(
        at == 0,
        jnp.sqrt(res2 / m),
        jnp.where(at == 1, (gain - by) / n, movement / jnp.sqrt(adx2 * dy2 + 1e-06)),
    )
    finish[-1].wait()


def publish(x_ref, y_ref, stats_ref, x_out, y_out, stats_out):
    x_out[...] = x_ref[...]
    y_out[...] = y_ref[...]
    stats_out[...] = stats_ref[:, :3]


def shards(grid, nrow, blocks, block_rows, block_cols, counts, x_prev, y_prev, cost, rhs, upper, steps):
    nx, ny, nz = grid
    nbd, bsz = blocks.shape[2], blocks.shape[3]
    rb = y_prev.shape[0] // bsz
    cb = x_prev.shape[0] // bsz
    ncol = nx * ny * nz
    vmem = pl.BlockSpec(memory_space=pltpu.VMEM)
    hbm = pl.BlockSpec(memory_space=pltpu.HBM)
    f32 = jnp.float32

    def buf(*shape):
        return pltpu.VMEM((*shape, LANES), f32)

    x_new, y_new, stats = pl.pallas_call(
        functools.partial(body, grid, nrow, nbd),
        out_shape=(
            pltpu.VMEM((cb, bsz), f32),
            pltpu.VMEM((rb, bsz), f32),
            pltpu.VMEM((1, LANES), f32),
        ),
        in_specs=[hbm] * 2 + [pl.BlockSpec(memory_space=pltpu.SMEM)] + [hbm] * 7,
        out_specs=(vmem, vmem, vmem),
        scratch_shapes=[
            pltpu.SMEM((1, 1, nbd), jnp.int32), pltpu.SMEM((1, 1, nbd), jnp.int32),
            pltpu.SMEM((2,), f32),
            buf(nbd, bsz), buf(cb), buf(rb), buf(cb), buf(rb), buf(cb),
            buf(nbd, bsz), buf(2, cb), buf(rb), pltpu.VMEM((nx, rb, ny * nz * nbd), jnp.bfloat16),
            buf(ny, 2 * nbd), buf(nx * nz, rb), buf(nx * nz, 1), buf(nrow, cb), buf(nrow, cb), buf(ncol, nbd), buf(rb),
            buf(ny, rb // ny), buf(ny, rb // ny), buf(nx * nz, rb // ny), buf(nx, 3 * cb), buf(nx, 1), buf(ny * nrow, 1), buf(nx * nrow, cb), buf(ny * nz, 1),
            pltpu.SemaphoreType.DMA((9,)),
            pltpu.SemaphoreType.DMA((14,)),
            pltpu.SemaphoreType.DMA((14,)),
            pltpu.SemaphoreType.REGULAR,
        ],
        compiler_params=pltpu.CompilerParams(collective_id=0, has_side_effects=True),
        name="pdlp",
    )(
        block_rows,
        block_cols,
        counts,
        steps,
        blocks.reshape(nbd, bsz, bsz),
        x_prev.reshape(cb, bsz),
        y_prev.reshape(rb, bsz),
        cost.reshape(cb, bsz),
        rhs.reshape(rb, bsz),
        upper.reshape(cb, bsz),
    )
    x_new, y_new, stats = pl.pallas_call(
        publish,
        out_shape=(
            jax.ShapeDtypeStruct((cb, bsz), f32),
            jax.ShapeDtypeStruct((rb, bsz), f32),
            jax.ShapeDtypeStruct((1, 3), f32),
        ),
        in_specs=[vmem] * 3,
        out_specs=(vmem,) * 3,
        name="publish",
    )(*(pltpu.with_memory_space_constraint(a, pltpu.VMEM) for a in (x_new, y_new, stats)))
    return x_new.reshape(-1), y_new.reshape(-1), stats.reshape(-1)


def solution(mesh):
    placed = (
        P("row", "col", None, None, None),
        P("row", "col", None),
        P("row", "col", None),
        P("row", "col"),
        P("col"),
        P("row"),
        P("col"),
        P("row"),
        P("col"),
        P(),
    )
    return jax.shard_map(
        functools.partial(shards, COL_GRID[mesh.shape["col"]], mesh.shape["row"]),
        mesh=mesh,
        in_specs=placed,
        out_specs=(P("col"), P("row"), P()),
        check_vma=False,
    )
```

```python
import functools

import jax
import jax.numpy as jnp
from jax import lax
from jax.experimental import pallas as pl
from jax.experimental.pallas import tpu as pltpu
from jax.sharding import PartitionSpec as P

MESH = pl.DeviceIdType.MESH
LANES = 128
NOWHERE = 1000.0
COL_GRID = {128: (2, 8, 8), 16: (2, 4, 2)}


def hops(d, n):
    return min(d, n - d)


def far_first(n):
    return sorted(range(1, n), key=lambda d: -hops(d, n))


def total(terms, op):
    acc = terms[0]
    for term in terms[1:]:
        acc = op(acc, term)
    return acc


def body(
    grid, nrow, nbd,
    brow_hbm, bcol_hbm, count_ref, steps_hbm, blocks_hbm, x_hbm, y_hbm, cost_hbm, rhs_hbm, upper_hbm,
    x_out, y_out, stats_out,
    brow_ref, bcol_ref, steps_ref, blocks_ref, vectors,
    flip_ref, vec_ref, scale_ref, hot_ref,
    max_y, max_q, code_q, cmax_buf, part_buf, fwd_buf, both_ref, move_send, move_y, move_q, half_buf, term_buf,
    dual_buf, back_buf, sum_buf,
    local_sems, send_sems, recv_sems, reached,
):
    nx, ny, nz = grid
    rb = y_hbm.shape[0]
    cb = x_hbm.shape[0]
    nq = nx * nz
    ncol = nq * ny
    qlanes = ny * nbd
    qper = min(LANES // qlanes, nz)
    width = qper * qlanes
    half = ny * nz
    share = rb // ny
    row = lax.axis_index("row")
    col = lax.axis_index("col")
    xh = lax.div(col, ny * nz)
    yi = lax.rem(lax.div(col, nz), ny)
    zi = lax.rem(col, nz)
    xs = [lax.rem(xh + d, nx) for d in range(nx)]
    ys = [lax.rem(yi + d, ny) for d in range(ny)]
    zs = [lax.rem(zi + d, nz) for d in range(nz)]
    rs = [lax.rem(row + d, nrow) for d in range(nrow)]
    place, core = lax.div(row, 2), lax.rem(row, 2)
    chips = [place]
    if nrow == 8:
        chips = [3 - place, lax.rem(place + 2, 4), place + 1 - 2 * lax.rem(place, 2), place]
    homes = [(chip * 2 + core, chip * 2 + 1 - core) for chip in chips]
    qi = xh * nz + zi
    slot = qi * ny + yi

    def col_device(d):
        dx, dy, dz = d
        return (row, (xs[dx] * ny + ys[dy]) * nz + zs[dz])

    def table_device(d):
        return (rs[d[1]], col_device((0, d[0], 0))[1])

    def ordered(offsets):
        cost = lambda d: (nx // 2) * 4 * d[0] + hops(d[1], ny) + hops(d[2], nz)
        return sorted(offsets, key=lambda d: -cost(d))

    line_y = [(0, d, 0) for d in far_first(ny)]
    line_z = [(0, 0, d) for d in far_first(nz)]
    plane = ordered([(a, 0, c) for a in range(nx) for c in range(nz) if a or c])
    everyone = ordered([(a, b, c) for a in range(nx) for b in range(ny) for c in range(nz) if a or b or c])
    sheet = [d for d in everyone if not d[0]]
    beyond = [d for d in everyone if d[0]]
    beside = col_device((1, 0, 0))[1]
    line_r = [(home, col) for pair in homes[:-1] for home in pair] + [(homes[-1][1], col)]
    ring = [(home, beside) for pair in homes[::-1] for home in pair]
    split = len(ring) // 2
    ring = ring[:split] + line_r[: split // 2] + ring[split:] + line_r[split // 2 :]
    partner = [col_device((1, 0, 0))]
    table = [(b, d) for b in far_first(ny) + [0] for d in far_first(nrow) + [0] if b or d]

    barrier = pltpu.get_barrier_semaphore()
    near = [col_device(d) for d in line_y] + line_r
    near += [col_device(d) for d in line_z] + [col_device((1, 0, 0))]
    lines = [(x_hbm, cb), (cost_hbm, cb), (upper_hbm, cb), (y_hbm, rb), (rhs_hbm, rb)]
    starts = [sum(n for _, n in lines[:i]) for i in range(len(lines))]
    x_ref, cost_ref, upper_ref, y_ref, rhs_ref = (
        vectors.at[pl.ds(start, n)] for start, (_, n) in zip(starts, lines)
    )
    fetches = [
        pltpu.make_async_copy(blocks_hbm, blocks_ref, local_sems.at[0]),
        pltpu.make_async_copy(brow_hbm, brow_ref, local_sems.at[1]),
        pltpu.make_async_copy(bcol_hbm, bcol_ref, local_sems.at[2]),
        pltpu.make_async_copy(steps_hbm, steps_ref, local_sems.at[3]),
    ]
    for (src, _), dst in zip(lines, (x_ref, cost_ref, upper_ref, y_ref, rhs_ref)):
        pltpu.make_async_copy(src, dst, local_sems.at[4]).start()
    late = [fetches[3], pltpu.make_async_copy(vectors, vectors, local_sems.at[4])]
    for copy in fetches:
        copy.start()
    for device in near:
        pl.semaphore_signal(barrier, inc=1, device_id=device, device_id_type=MESH)
    finish = []

    def send(at, peers, buf, me, sources=None):
        for i, device in enumerate(peers):
            pltpu.make_async_remote_copy(
                src_ref=sources[i] if sources else buf.at[me],
                dst_ref=buf.at[me],
                send_sem=send_sems.at[at],
                recv_sem=recv_sems.at[at],
                device_id=device,
                device_id_type=MESH,
            ).start()
        theirs = buf.at[pl.ds(0, len(peers))]
        finish.append(pltpu.make_async_copy(theirs, theirs, send_sems.at[at]))
        return pltpu.make_async_copy(theirs, theirs, recv_sems.at[at]).wait

    def whole(buf, op):
        return total([buf[i] for i in range(buf.shape[0])], op)

    for copy in fetches[:3]:
        copy.wait()
    count = count_ref[0, 0]
    brow = [brow_ref[0, 0, k] for k in range(nbd)]
    bcol = [bcol_ref[0, 0, k] for k in range(nbd)]
    rows = [jnp.where(k < count, brow[k].astype(jnp.float32), NOWHERE) for k in range(nbd)]
    cols = [jnp.where(k < count, bcol[k], -1) for k in range(nbd)]
    tile_at = lax.broadcasted_iota(jnp.int32, (2 * nbd, LANES), 0)
    cb_at = lax.broadcasted_iota(jnp.int32, (cb, LANES), 0)

    def stacked(entries):
        out = jnp.zeros((len(entries), LANES), jnp.float32)
        for i, entry in enumerate(entries):
            out = jnp.where(tile_at == i, entry, out)
        return out

    col_peak = jnp.zeros((cb, LANES), jnp.float32)
    row_peaks = []
    for k in range(nbd):
        block = blocks_ref[k]
        flip = block.T
        flip_ref[k] = flip
        row_peaks.append(jnp.max(jnp.abs(flip), axis=0, keepdims=True))
        peak = jnp.max(jnp.abs(block), axis=0, keepdims=True)
        col_peak = jnp.maximum(col_peak, jnp.where(cb_at == cols[k], peak, 0.0))
    max_y[yi] = stacked(row_peaks + rows)
    cmax_buf[row] = col_peak
    pl.semaphore_wait(barrier, len(near))
    pl.semaphore_signal(reached, inc=1, device_id=col_device((1, 0, 0)), device_id_type=MESH)
    arrive = send(0, [col_device(d) for d in line_y], max_y, yi)
    arrive_c = send(1, line_r, cmax_buf, row)
    for copy in late:
        copy.wait()
    rb_at = lax.broadcasted_iota(jnp.int32, (rb, LANES), 0).astype(jnp.float32)
    lane = lax.broadcasted_iota(jnp.int32, (2 * nbd, LANES), 1)
    mine = (lane // qlanes == lax.rem(qi, qper)) & (tile_at - nbd == lane % nbd)
    owner = lane % qlanes // nbd
    arrive()
    dense = jnp.zeros((rb, LANES), jnp.float32)
    for j in range(ny):
        for k in range(nbd):
            here = rb_at == max_y[j, nbd + k : nbd + k + 1]
            dense = jnp.maximum(dense, jnp.where(here, max_y[j, k : k + 1], 0.0))
    max_q[qi] = dense
    pl.semaphore_wait(reached, 1)
    arrive = send(2, [col_device(d) for d in plane], max_q, qi)
    codes = jnp.zeros((2 * nbd, LANES), jnp.float32)
    for j in range(ny):
        codes = jnp.where(mine & (owner == j), max_y[j], codes)
    code_q[qi] = jnp.sum(codes, axis=0, keepdims=True)
    arrive_code = send(3, [col_device(d) for d in plane], code_q, qi)
    arrive_c()
    col_scale = 1.0 / jnp.sqrt(jnp.maximum(whole(cmax_buf, jnp.maximum), 0.5))
    cost_s = col_scale * cost_ref[...]
    upper_s = upper_ref[...] / col_scale
    x_prev = x_ref[...]
    eta = steps_ref[0]
    omega = steps_ref[1]
    omega_v = jnp.full((1, 1), omega)
    tau = eta / omega_v
    sigma = eta * omega
    arrive()
    rowmax = whole(max_q, jnp.maximum)
    row_scale = 1.0 / jnp.sqrt(jnp.maximum(rowmax, 0.5))
    scale_ref[...] = row_scale

    def backward(ref):
        got = [ref[pl.ds(brow[k], 1), :] * scale_ref[pl.ds(brow[k], 1), :] for k in range(nbd)]
        vec = stacked(got + got).T
        out = jnp.zeros((cb, LANES), jnp.float32)
        for k in range(nbd):
            prod = jnp.sum(blocks_ref[k] * vec[:, k : k + 1], axis=0, keepdims=True)
            out = out + jnp.where(cb_at == cols[k], prod, 0.0)
        return out

    part_buf[row] = backward(y_ref)
    arrive = send(12, line_r, part_buf, row)
    half_buf[xh, :cb] = cost_s
    half_buf[xh, cb : 2 * cb] = upper_s
    half_buf[xh, 2 * cb :] = col_scale
    arrive_half = send(4, partner, half_buf, xh)
    arrive_code()
    for g in range(nq // qper):
        code = total([code_q[i] for i in range(g * qper, (g + 1) * qper)], jnp.add)
        h, start = divmod(g * width, half * nbd)
        hot_ref[h, :, start : start + width] = jnp.where(rb_at == code, 1.0, 0.0).astype(jnp.bfloat16)[:, :width]
    rhs_s = row_scale * rhs_ref[...]
    arrive()
    grad = cost_s - whole(part_buf, jnp.add) * col_scale
    x_new = jnp.clip(x_prev - tau * grad, 0.0, upper_s)
    delta_x = x_new - x_prev
    vec_ref[0] = (x_new + delta_x) * col_scale
    vec_ref[1] = delta_x * col_scale

    vecs = stacked([vec_ref[v, pl.ds(bcol[k], 1), :] for v in range(2) for k in range(nbd)]).T

    def forward(v):
        return [
            jnp.sum(flip_ref[k] * vecs[:, v * nbd + k : v * nbd + k + 1], axis=0, keepdims=True) for k in range(nbd)
        ]

    def gathered(ref, h):
        rest = ref[pl.ds(h * half, half)].reshape(half * nbd, LANES)
        hot = hot_ref[h]
        out = jnp.zeros((rb, LANES), jnp.float32)
        for _ in range(3):
            part = rest.astype(jnp.bfloat16)
            rest = rest - part.astype(jnp.float32)
            out = out + jnp.dot(hot, part, preferred_element_type=jnp.float32)
        return out

    def folded(term):
        out = jnp.sum(term, axis=0, keepdims=True)
        return out + pltpu.roll(out, LANES // 2, 1)

    prods = forward(0)
    fwd_buf[slot] = stacked(prods + prods)[:nbd]
    arrive_far = send(5, [col_device(d) for d in beyond], fwd_buf, slot)
    prods = forward(1)
    share_at = lax.broadcasted_iota(jnp.int32, (share, LANES), 0).astype(jnp.float32)
    for j in range(ny):
        move_send[j] = total([jnp.where(share_at + j * share == rows[k], prods[k], 0.0) for k in range(nbd)], jnp.add)
    move_y[yi] = move_send[yi]
    arrive_move = send(6, [col_device(d) for d in line_y], move_y, yi, [move_send.at[ys[d[1]]] for d in line_y])
    arrive = send(11, [col_device(d) for d in sheet], fwd_buf, slot)
    left = lax.broadcasted_iota(jnp.int32, (1, LANES), 1) < LANES // 2
    term_buf[xh] = jnp.where(left, folded(delta_x * delta_x), folded(cost_s * x_new))
    arrive_term = send(7, partner, term_buf, xh)
    x_out[...] = x_new
    y_prev = y_ref[...]
    arrive_move()
    move_q[qi] = whole(move_y, jnp.add)
    arrive_move = send(13, [col_device(d) for d in plane], move_q, qi)
    arrive()
    both = gathered(fwd_buf, xh)
    arrive_far()
    both = (both + gathered(fwd_buf, 1 - xh)) * row_scale
    both_ref[...] = rhs_s - both
    y_new = y_prev + sigma * (rhs_s - both)
    y_out[...] = y_new
    mine_at = xh * nrow + row
    back_buf[mine_at] = backward(y_out)
    arrive = send(8, ring, back_buf, mine_at)
    arrive_move()
    at = pl.ds(pl.multiple_of(yi * share, share), share)
    scale = scale_ref[at, :]
    adx = whole(move_q, jnp.add) * scale
    y_share = y_out[at, :]
    delta_y = y_share - y_ref[at, :]
    resid = both_ref[at, :] + adx
    quarter = lax.broadcasted_iota(jnp.int32, (1, LANES), 1) // (LANES // 4)
    duals = jnp.zeros((1, LANES), jnp.float32)
    for i, term in enumerate((delta_y * delta_y, adx * adx, resid * resid, scale * rhs_ref[at, :] * y_share)):
        term = folded(term)
        duals = jnp.where(quarter == i, term + pltpu.roll(term, LANES // 4, 1), duals)
    spot = yi * nrow + row
    dual_buf[spot] = duals
    arrive_dual = send(10, [table_device(d) for d in table], dual_buf, spot)
    arrive_half()
    arrive_term()
    terms = total([term_buf[h] for h in range(nx)], jnp.add)
    arrive()
    gains = []
    for h in range(nx):
        product = total([back_buf[h * nrow + r] for r in range(nrow)], jnp.add)
        reduced = half_buf[h, :cb] - product * half_buf[h, 2 * cb :]
        gains.append(folded(half_buf[h, cb : 2 * cb] * jnp.maximum(-reduced, 0.0)))
    spot = yi * nz + zi
    sum_buf[spot] = terms + jnp.where(left, 0.0, total(gains, jnp.add))
    arrive = send(9, [col_device(d) for d in sheet], sum_buf, spot)
    for copy in finish[:-1]:
        copy.wait()
    arrive_dual()
    dual = whole(dual_buf, jnp.add)
    dy2, adx2, res2, by = (jnp.sum(jnp.where(quarter == i, dual, 0.0), axis=1, keepdims=True) for i in range(4))
    m = rb * LANES * nrow
    n = cb * LANES * ncol
    arrive()
    primal = whole(sum_buf, jnp.add)
    dx2 = jnp.sum(jnp.where(left, primal, 0.0), axis=1, keepdims=True)
    gain = jnp.sum(jnp.where(left, 0.0, primal), axis=1, keepdims=True)
    movement = 0.5 * omega * dx2 + 0.5 / omega_v * dy2
    at = lax.broadcasted_iota(jnp.int32, (1, LANES), 1)
    stats_out[...] = jnp.where(
        at == 0,
        jnp.sqrt(res2 / m),
        jnp.where(at == 1, (gain - by) / n, movement / jnp.sqrt(adx2 * dy2 + 1e-06)),
    )
    finish[-1].wait()


def publish(x_ref, y_ref, stats_ref, x_out, y_out, stats_out):
    x_out[...] = x_ref[...]
    y_out[...] = y_ref[...]
    stats_out[...] = stats_ref[:, :3]


def shards(grid, nrow, blocks, block_rows, block_cols, counts, x_prev, y_prev, cost, rhs, upper, steps):
    nx, ny, nz = grid
    nbd, bsz = blocks.shape[2], blocks.shape[3]
    rb = y_prev.shape[0] // bsz
    cb = x_prev.shape[0] // bsz
    ncol = nx * ny * nz
    vmem = pl.BlockSpec(memory_space=pltpu.VMEM)
    hbm = pl.BlockSpec(memory_space=pltpu.HBM)
    f32 = jnp.float32

    def buf(*shape):
        return pltpu.VMEM((*shape, LANES), f32)

    x_new, y_new, stats = pl.pallas_call(
        functools.partial(body, grid, nrow, nbd),
        out_shape=(
            pltpu.VMEM((cb, bsz), f32),
            pltpu.VMEM((rb, bsz), f32),
            pltpu.VMEM((1, LANES), f32),
        ),
        in_specs=[hbm] * 2 + [pl.BlockSpec(memory_space=pltpu.SMEM)] + [hbm] * 7,
        out_specs=(vmem, vmem, vmem),
        scratch_shapes=[
            pltpu.SMEM((1, 1, nbd), jnp.int32), pltpu.SMEM((1, 1, nbd), jnp.int32),
            pltpu.SMEM((2,), f32),
            buf(nbd, bsz), buf(3 * cb + 2 * rb),
            buf(nbd, bsz), buf(2, cb), buf(rb), pltpu.VMEM((nx, rb, ny * nz * nbd), jnp.bfloat16),
            buf(ny, 2 * nbd), buf(nx * nz, rb), buf(nx * nz, 1), buf(nrow, cb), buf(nrow, cb), buf(ncol, nbd), buf(rb),
            buf(ny, rb // ny), buf(ny, rb // ny), buf(nx * nz, rb // ny), buf(nx, 3 * cb), buf(nx, 1), buf(ny * nrow, 1), buf(nx * nrow, cb), buf(ny * nz, 1),
            pltpu.SemaphoreType.DMA((5,)),
            pltpu.SemaphoreType.DMA((14,)),
            pltpu.SemaphoreType.DMA((14,)),
            pltpu.SemaphoreType.REGULAR,
        ],
        compiler_params=pltpu.CompilerParams(collective_id=0, has_side_effects=True),
        name="pdlp",
    )(
        block_rows,
        block_cols,
        counts,
        steps,
        blocks.reshape(nbd, bsz, bsz),
        x_prev.reshape(cb, bsz),
        y_prev.reshape(rb, bsz),
        cost.reshape(cb, bsz),
        rhs.reshape(rb, bsz),
        upper.reshape(cb, bsz),
    )
    x_new, y_new, stats = pl.pallas_call(
        publish,
        out_shape=(
            jax.ShapeDtypeStruct((cb, bsz), f32),
            jax.ShapeDtypeStruct((rb, bsz), f32),
            jax.ShapeDtypeStruct((1, 3), f32),
        ),
        in_specs=[vmem] * 3,
        out_specs=(vmem,) * 3,
        name="publish",
    )(*(pltpu.with_memory_space_constraint(a, pltpu.VMEM) for a in (x_new, y_new, stats)))
    return x_new.reshape(-1), y_new.reshape(-1), stats.reshape(-1)


def solution(mesh):
    placed = (
        P("row", "col", None, None, None),
        P("row", "col", None),
        P("row", "col", None),
        P("row", "col"),
        P("col"),
        P("row"),
        P("col"),
        P("row"),
        P("col"),
        P(),
    )
    return jax.shard_map(
        functools.partial(shards, COL_GRID[mesh.shape["col"]], mesh.shape["row"]),
        mesh=mesh,
        in_specs=placed,
        out_specs=(P("col"), P("row"), P()),
        check_vma=False,
    )
```
